32 devices in a mesh: row: 8 (over z, x), col: 4 (over y, core).
Axes of the slice: x: 2, y: 2, z: 4, core: 2. Of those that a mesh axis runs over, the one named last changes fastest.
Arguments:
- resident_inverse: float32 [12288, 12288], P('row', 'col'), as said below
- factor_panel: float32 [2, 12288, 256], P(None, 'row', 'col'), may hold values from -0.109375 to 0.109375
- diag_inverse: float32 [2, 256, 256], P(None, 'row', 'col'), as said below
- ancestors: int32 [2, 48], replicated, may hold values from 0 to 1, as said below
- start_order: int32 [2], replicated, may hold values from 0 to 1, each once
Outputs:
- inverse_column: float32 [2, 12288, 256], P(None, 'row', 'col')
- inverse_row: float32 [2, 256, 12288], P(None, 'row', 'col')
- diagonal_block: float32 [2, 256, 256], P(None, 'row', 'col')
The draws below stay inside these ranges and needn't reach their ends.
Inputs may be any that keep to these rules, and one draw needn't show every extreme that they name: `ancestors`: 1 marks a tile of 256 rows among the supernode's ancestor rows; each supernode marks between 32 and 48 tiles. `start_order`: a permutation of the supernodes. `resident_inverse`: symmetric. `diag_inverse`: each supernode's block is symmetric.
All inputs are finite; a program needn't handle non-finite values.
Results may differ from the reference program's by a relative error of at most 0.0001.
Values sent between devices are 32-bit elements; how exact they have to be, the bound alone decides.
No kernel may reach another device: no remote copies, remote signals or barrier semaphores. Data moves between devices by JAX's collectives and lax.ppermute only.
A program may use at most 64 MiB of HBM per device.

```python
import math
import jax
import jax.numpy as jnp
from jax import lax

ORD = 12288
W = 256
TILE = 256
SUPER = 2
NT = 48


def draw_resident_inverse(key, part):
    off_key = jax.random.fold_in(key, 11)
    diag_key = jax.random.fold_in(key, 12)
    entries = jax.random.normal(off_key, (ORD, ORD), jnp.float32)
    symmetric = (entries + entries.T) * (0.70710678 / math.sqrt(ORD))
    diagonal = 3.0 + 2.0 * jax.random.uniform(diag_key, (ORD,), jnp.float32)
    positions = jnp.arange(ORD)
    return symmetric.at[positions, positions].set(diagonal)


def draw_diag_inverse(key, part):
    off_key = jax.random.fold_in(key, 21)
    diag_key = jax.random.fold_in(key, 22)
    entries = jax.random.normal(off_key, (SUPER, W, W), jnp.float32)
    symmetric = (entries + jnp.swapaxes(entries, 1, 2)) * (0.70710678 * 0.7 / math.sqrt(W))
    diagonal = 2.0 + 1.5 * jax.random.uniform(diag_key, (SUPER, W), jnp.float32)
    return symmetric + jnp.eye(W, dtype=jnp.float32)[None, :, :] * diagonal[:, :, None]


def draw_ancestors(key, part):
    count_key = jax.random.fold_in(key, 31)
    score_key = jax.random.fold_in(key, 32)
    counts = jax.random.randint(count_key, (SUPER, 1), 2 * NT // 3, NT + 1)
    noise = jax.random.randint(score_key, (SUPER, NT), 0, NT)
    tiles = jnp.arange(NT, dtype=jnp.int32)[None, :]
    scores = (noise + 2 * tiles) * NT + tiles
    ranking = jnp.argsort(jnp.argsort(-scores, axis=1), axis=1)
    return (ranking < counts).astype(jnp.int32)


def steps_of(stream_key, shape, shards, smallest, largest):
    def one(axis_at, blocks):
        heights = jax.random.uniform(jax.random.fold_in(jax.random.fold_in(stream_key, 6), axis_at), (blocks,), jnp.float32, smallest / len(shards), largest / len(shards))
        return jnp.repeat(jnp.exp(heights), shape[axis_at] // blocks).reshape((-1,) + (1,) * (len(shape) - axis_at - 1))

    loudness = one(*shards[0])
    for cut in shards[1:]:
        loudness = loudness * one(*cut)
    return loudness


def centred(key, dims, spread, bound, pieces=(), held_as=jnp.bfloat16):
    array = jax.random.normal(key, dims, jnp.float32) * spread
    if len(pieces) > 0:
        array = steps_of(key, dims, pieces, -0.22, 0.18) * array
    return jnp.clip(array, min=-bound, max=bound).astype(held_as)


def setup_inputs(seed: int = 0) -> dict:
    splits = jax.random.split(jax.random.key(seed), 6)
    resident_inverse = draw_resident_inverse(jax.random.fold_in(splits[5], 71), 0)
    factor_panel = centred(splits[1], (SUPER, ORD, W), (ORD // 4) ** -0.5, 0.109375, ((1, 8), (2, 4)), jnp.float32)
    diag_inverse = draw_diag_inverse(jax.random.fold_in(splits[5], 71), 0)
    ancestors = draw_ancestors(jax.random.fold_in(splits[5], 71), 0)
    start_order = jax.random.permutation(splits[4], SUPER).astype(jnp.int32)
    return dict(resident_inverse=resident_inverse, factor_panel=factor_panel, diag_inverse=diag_inverse, ancestors=ancestors, start_order=start_order)


def reference(resident_inverse, factor_panel, diag_inverse, ancestors, start_order):
    columns = []
    transposed_rows = []
    blocks = []
    for section_index in range(SUPER):
        chosen = start_order[section_index]
        tile_flags = jnp.repeat(ancestors[chosen], TILE).astype(jnp.float32)
        masked = factor_panel[chosen] * tile_flags[:, None]
        column = -tile_flags[:, None] * jnp.dot(resident_inverse, masked, precision=lax.Precision.HIGHEST)
        transposed = -jnp.dot(masked.T, resident_inverse, precision=lax.Precision.HIGHEST) * tile_flags[None, :]
        diagonal = diag_inverse[chosen] - jnp.dot(masked.T, column, precision=lax.Precision.HIGHEST)
        columns.append(column)
        transposed_rows.append(transposed)
        blocks.append(diagonal)
    return jnp.stack(columns), jnp.stack(transposed_rows), jnp.stack(blocks)
```

```python
import functools
import jax
import jax.numpy as jnp
from jax import lax
from jax.experimental import pallas as pl
from jax.experimental.pallas import tpu as pltpu
from jax.sharding import PartitionSpec as P

INNER = 2
GROUPED = False


def swap_bit(block, axis, bit):
    count = lax.axis_size(axis)
    return lax.ppermute(block, axis, [(i, i ^ (1 << bit)) for i in range(count)])


def split(values):
    high = values.astype(jnp.bfloat16)
    return high, (values - high.astype(jnp.float32)).astype(jnp.bfloat16)


def dot(left, right, contract):
    return lax.dot_general(left, right, (contract, ((), ())), preferred_element_type=jnp.float32)


def mask_kernel(tile, order_ref, flags_ref, place_ref, panel_ref, out_ref):
    section = order_ref[pl.program_id(0)]
    for t in range(panel_ref.shape[2] // tile):
        flag = flags_ref[section, place_ref[0] + t].astype(jnp.float32)
        at = pl.ds(t * tile, tile)
        out_ref[0, :, at] = panel_ref[0, :, at] * flag


def masked_panels(panel, ancestors, start_order, first_tile, tile):
    sections, width, rows = panel.shape
    return pl.pallas_call(
        functools.partial(mask_kernel, tile),
        grid_spec=pltpu.PrefetchScalarGridSpec(
            num_scalar_prefetch=3,
            grid=(sections,),
            in_specs=[pl.BlockSpec((1, width, rows), lambda s, order, flags, place: (order[s], 0, 0))],
            out_specs=pl.BlockSpec((1, width, rows), lambda s, order, flags, place: (s, 0, 0)),
        ),
        out_shape=jax.ShapeDtypeStruct(panel.shape, jnp.float32),
        compiler_params=pltpu.CompilerParams(vmem_limit_bytes=8 << 20),
        cost_estimate=pl.CostEstimate(flops=panel.size, bytes_accessed=8 * panel.size, transcendentals=0),
        name="mask_panels",
    )(start_order, ancestors, first_tile, panel)


def terms_kernel(dims, table_ref, inverse_ref, *refs):
    pieces_count, ratio, narrow, steps, members = dims
    pieces, refs = refs[:pieces_count], refs[pieces_count:]
    sends, (kept_ref, high_ref, low_ref, left_ref) = refs[:steps], refs[steps:]
    h = pl.program_id(0)
    n = pl.program_id(1)
    rows = members * steps * INNER * narrow

    @pl.when((h == 0) & (n == 0))
    def _():
        for m in range(pieces_count):
            for g in range(members):
                for l in range(ratio):
                    high, low = split(pieces[m][g, l * narrow : (l + 1) * narrow, :])
                    high_ref[m * ratio + l, g] = high
                    low_ref[m * ratio + l, g] = low

    @pl.when(n == 0)
    def _():
        for j in range(steps):
            for i in range(INNER):
                unit = table_ref[h, j * INNER + i]
                for g in range(members):
                    at = ((g * steps + j) * INNER + i) * narrow
                    left_ref[at : at + narrow, :] = high_ref[unit, g]
                    left_ref[rows + at : rows + at + narrow, :] = low_ref[unit, g]

    high, low = split(inverse_ref[...])
    both = dot(left_ref[...], high, ((1,), (0,)))
    total = both[:rows] + both[rows:] + dot(left_ref[:rows, :], low, ((1,), (0,)))
    total = total.reshape(members, steps, INNER, narrow, total.shape[1])
    for g in range(members):
        for j in range(steps):
            sends[j][g, 0] = total[g, j, 0]
            kept_ref[j, g, 0] = total[g, j, 1]


def panel_terms(table, inverse, pieces, ratio):
    members, width, rows = pieces[0].shape
    count = len(pieces)
    steps = table.shape[1] // INNER
    narrow = width // ratio
    half = inverse.shape[1] // 2
    tiles = next(t for t in range(1, half + 1) if half % t == 0 and half // t <= 512)
    block = half // tiles
    lefts = members * steps * INNER * narrow
    whole = pl.BlockSpec((members, width, rows), lambda h, n, table: (0, 0, 0))
    flops = 6 * lefts * inverse.size
    outs = pl.pallas_call(
        functools.partial(terms_kernel, (count, ratio, narrow, steps, members)),
        grid_spec=pltpu.PrefetchScalarGridSpec(
            num_scalar_prefetch=1,
            grid=(2, tiles),
            in_specs=[pl.BlockSpec((rows, block), lambda h, n, table: (0, h * tiles + n))] + [whole] * count,
            out_specs=[pl.BlockSpec((members, 1, narrow, block), lambda h, n, table: (0, h, 0, n))] * steps
            + [pl.BlockSpec((steps, members, 1, narrow, block), lambda h, n, table: (0, 0, h, 0, n))],
            scratch_shapes=[
                pltpu.VMEM((count * ratio, members, narrow, rows), jnp.bfloat16),
                pltpu.VMEM((count * ratio, members, narrow, rows), jnp.bfloat16),
                pltpu.VMEM((2 * lefts, rows), jnp.bfloat16),
            ],
        ),
        out_shape=[jax.ShapeDtypeStruct((members, 2, narrow, half), jnp.float32)] * steps
        + [jax.ShapeDtypeStruct((steps, members, 2, narrow, half), jnp.float32)],
        compiler_params=pltpu.CompilerParams(vmem_limit_bytes=32 << 20),
        cost_estimate=pl.CostEstimate(flops=flops, bytes_accessed=4 * inverse.size, transcendentals=0),
        name="panel_terms",
    )(table, inverse, *pieces)
    return outs[:steps], outs[steps]


def gather_pieces(block):
    count = lax.axis_size("col")
    pieces = {0: block}
    for bit in reversed(range(count.bit_length() - 1)):
        for held, piece in list(pieces.items()):
            pieces[held ^ (1 << bit)] = swap_bit(piece, "col", bit)
    return [pieces[i] for i in range(count)]


def mirror_routes(row_count, col_count, shift):
    ratio = row_count // col_count
    straight, first, second = [], [], []
    for r in range(row_count):
        for c in range(col_count):
            target = (c * ratio + (r % ratio + shift) % ratio, r // ratio)
            middle = (r, target[1] // 2 * 2 + c % 2)
            if shift == 0 or middle[1] == c:
                straight.append(((r, c), target))
            else:
                first.append(((r, c), middle))
                second.append((middle, target))
    if len(set(m for _, m in first)) != len(first):
        straight += [(f[0], s[1]) for f, s in zip(first, second)]
        first, second = [], []
    flat = lambda pairs: [(a[0] * col_count + a[1], b[0] * col_count + b[1]) for a, b in pairs]
    return flat(straight), flat(first), flat(second)


def mirrored(pieces):
    row_count = lax.axis_size("row")
    col_count = lax.axis_size("col")
    ratio = row_count // col_count
    lower = lax.axis_index("row") % ratio
    arrived = []
    for shift in range(ratio):
        straight, first, second = mirror_routes(row_count, col_count, shift)
        piece = pieces[(0 + shift) % ratio]
        for l in range(1, ratio):
            piece = jnp.where(lower == l, pieces[(l + shift) % ratio], piece)
        got = lax.ppermute(piece, ("row", "col"), straight)
        if first:
            got = got + lax.ppermute(lax.ppermute(piece, ("row", "col"), first), ("row", "col"), second)
        arrived.append(got)
    return arrived


def unmirror(arrived, axis):
    ratio = len(arrived)
    lower = lax.axis_index("row") % ratio
    placed = []
    for source in range(ratio):
        piece = arrived[(0 - source) % ratio]
        for l in range(1, ratio):
            piece = jnp.where(lower == l, arrived[(l - source) % ratio], piece)
        placed.append(piece)
    return jnp.concatenate(placed, axis=axis)


def diag_kernel(count, column_ref, *refs):
    pieces, out_ref = refs[:count], refs[count]
    width = pieces[0].shape[1]
    for g in range(out_ref.shape[0]):
        high, low = split(column_ref[g])
        for m in range(count):
            left_high, left_low = split(pieces[m][g])
            left = jnp.concatenate([left_high, left_low], axis=0)
            both = dot(left, high, ((1,), (1,)))
            out_ref[g, m] = both[:width] + both[width:] + dot(left_high, low, ((1,), (1,)))


def diag_terms(column, pieces):
    members, width, rows = column.shape
    count = len(pieces)
    return pl.pallas_call(
        functools.partial(diag_kernel, count),
        out_shape=jax.ShapeDtypeStruct((members, count, width, width), jnp.float32),
        compiler_params=pltpu.CompilerParams(vmem_limit_bytes=16 << 20),
        cost_estimate=pl.CostEstimate(
            flops=6 * members * count * width * width * rows,
            bytes_accessed=4 * members * (count + 1) * width * rows,
            transcendentals=0,
        ),
        name="diag_terms",
    )(column, *pieces)


def on_device(resident_inverse, factor_panel, diag_inverse, ancestors, start_order):
    row_count = lax.axis_size("row")
    col_count = lax.axis_size("col")
    row_index = lax.axis_index("row")
    col_index = lax.axis_index("col")
    rows_here, cols_here = resident_inverse.shape
    sections, _, slice_width = factor_panel.shape
    tile = rows_here * row_count // ancestors.shape[1]
    ratio = row_count // col_count
    narrow = slice_width // ratio
    steps = row_count // INNER
    outer = row_index // INNER
    inner = row_index % INNER
    half = cols_here // 2

    first_tile = (row_index * (rows_here // tile)).astype(jnp.int32).reshape(1)
    own = masked_panels(jnp.swapaxes(factor_panel, 1, 2), ancestors, start_order, first_tile, tile)

    tiles_here = cols_here // tile
    flags = lax.dynamic_slice_in_dim(ancestors, col_index * tiles_here, tiles_here, 1)
    flags = jnp.where((start_order == 0)[:, None], flags[:1], flags[1:]) if sections == 2 else flags[start_order]
    col_masks = jnp.repeat(flags.astype(jnp.float32), tile, axis=1)

    turns = jnp.arange(steps)
    outers = jnp.stack([(outer - 1 - turns) % steps, (outer + 1 + turns) % steps])
    rows_wanted = outers[:, :, None] * INNER + jnp.stack([1 - inner, inner])[None, None, :]
    table = ((rows_wanted // ratio) ^ col_index) * ratio + rows_wanted % ratio
    table = table.reshape(2, steps * INNER).astype(jnp.int32)

    groups = [list(range(sections))] if GROUPED else [[s] for s in range(sections)]
    forward = [(r, (r + INNER) % row_count) for r in range(row_count)]
    backward = [(b, a) for a, b in forward]
    across = [(r, r ^ 1) for r in range(row_count)]

    gathered = [gather_pieces(own[g[0] : g[-1] + 1]) for g in groups]

    row_results, col_results, diag_parts = [], [], []
    for members, pieces in zip(groups, gathered):
        sends, kept = panel_terms(table, resident_inverse, pieces, ratio)
        carry = [None, None]
        for step in range(steps):
            arrived = lax.ppermute(sends[step], "row", across)
            for h in range(2):
                here = kept[step, :, h] + arrived[:, h]
                if step:
                    here = here + lax.ppermute(carry[h], "row", forward if h == 0 else backward)
                carry[h] = here
        masks = col_masks[members[0] : members[-1] + 1, None, :]
        finished = [-carry[h] * masks[:, :, h * half : (h + 1) * half] for h in range(2)]
        if ratio == 2:
            turned = mirrored(finished)
        else:
            joined = jnp.concatenate(finished, axis=-1)
            turned = mirrored([joined[:, :, q * rows_here : (q + 1) * rows_here] for q in range(ratio)])
        row_results.append(jnp.concatenate(finished, axis=-1))
        column = unmirror(turned, 1)
        col_results.append(column)
        diag_parts.append(diag_terms(column, pieces))

    rest = jnp.concatenate(diag_parts, axis=0).reshape(sections, row_count, narrow, slice_width)
    place = ((row_index // ratio) ^ col_index) * ratio + row_index % ratio
    for bit in range(row_count.bit_length() - 1):
        own_bit = (place >> bit) & 1
        shaped = rest.reshape(sections, -1, 2, narrow, slice_width)
        outgoing = lax.dynamic_index_in_dim(shaped, 1 - own_bit, 2, keepdims=False)
        stays = lax.dynamic_index_in_dim(shaped, own_bit, 2, keepdims=False)
        rest = stays + swap_bit(outgoing, "row", bit)
    if sections == 2:
        flipped = jnp.flip(diag_inverse, axis=0)
        sectioned_diag = jnp.where(start_order[0] == 0, diag_inverse, flipped)
    else:
        sectioned_diag = jnp.take(diag_inverse, start_order, axis=0)
    diag_result = sectioned_diag - rest.reshape(sections, narrow, slice_width)

    col_out = jnp.swapaxes(jnp.concatenate(col_results, axis=0), 1, 2)
    return (col_out, jnp.concatenate(row_results, axis=0), diag_result)


def solution(mesh):
    return jax.shard_map(
        on_device,
        mesh=mesh,
        in_specs=(P("row", "col"), P(None, "row", "col"), P(None, "row", "col"), P(), P()),
        out_specs=(P(None, "row", "col"), P(None, "row", "col"), P(None, "row", "col")),
        check_vma=False,
    )
```

```python
import functools
import jax
import jax.numpy as jnp
from jax import lax
from jax.experimental import pallas as pl
from jax.experimental.pallas import tpu as pltpu
from jax.sharding import PartitionSpec as P

INNER = 2


def swap_bit(block, axis, bit):
    count = lax.axis_size(axis)
    return lax.ppermute(block, axis, [(i, i ^ (1 << bit)) for i in range(count)])


def split(values):
    high = values.astype(jnp.bfloat16)
    return high, (values - high.astype(jnp.float32)).astype(jnp.bfloat16)


def dot(left, right, contract):
    return lax.dot_general(left, right, (contract, ((), ())), preferred_element_type=jnp.float32)


def mask_kernel(tile, order_ref, flags_ref, place_ref, panel_ref, out_ref):
    section = order_ref[pl.program_id(0)]
    for t in range(panel_ref.shape[2] // tile):
        flag = flags_ref[section, place_ref[0] + t].astype(jnp.float32)
        at = pl.ds(t * tile, tile)
        out_ref[0, :, at] = panel_ref[0, :, at] * flag


def masked_panels(panel, ancestors, start_order, first_tile, tile):
    sections, width, rows = panel.shape
    return pl.pallas_call(
        functools.partial(mask_kernel, tile),
        grid_spec=pltpu.PrefetchScalarGridSpec(
            num_scalar_prefetch=3,
            grid=(sections,),
            in_specs=[pl.BlockSpec((1, width, rows), lambda s, order, flags, place: (order[s], 0, 0))],
            out_specs=pl.BlockSpec((1, width, rows), lambda s, order, flags, place: (s, 0, 0)),
        ),
        out_shape=jax.ShapeDtypeStruct(panel.shape, jnp.float32),
        compiler_params=pltpu.CompilerParams(vmem_limit_bytes=8 << 20),
        cost_estimate=pl.CostEstimate(flops=panel.size, bytes_accessed=8 * panel.size, transcendentals=0),
        name="mask_panels",
    )(start_order, ancestors, first_tile, panel)


def column_block(columns):
    return next(columns // t for t in range(1, columns + 1) if columns % t == 0 and columns // t <= 512)


def terms_kernel(dims, table_ref, inverse_ref, *refs):
    pieces_count, ratio, narrow, steps, members = dims
    pieces, refs = refs[:pieces_count], refs[pieces_count:]
    sends, (kept_ref, high_ref, low_ref, left_ref) = refs[:steps], refs[steps:]
    h = pl.program_id(0)
    n = pl.program_id(1)
    rows = members * steps * INNER * narrow

    @pl.when((h == 0) & (n == 0))
    def _():
        for m in range(pieces_count):
            for g in range(members):
                for l in range(ratio):
                    high, low = split(pieces[m][g, l * narrow : (l + 1) * narrow, :])
                    high_ref[m * ratio + l, g] = high
                    low_ref[m * ratio + l, g] = low

    @pl.when(n == 0)
    def _():
        for j in range(steps):
            for i in range(INNER):
                unit = table_ref[h, j * INNER + i]
                for g in range(members):
                    at = ((g * steps + j) * INNER + i) * narrow
                    left_ref[at : at + narrow, :] = high_ref[unit, g]
                    left_ref[rows + at : rows + at + narrow, :] = low_ref[unit, g]

    high, low = split(inverse_ref[...])
    both = dot(left_ref[...], high, ((1,), (0,)))
    total = both[:rows] + both[rows:] + dot(left_ref[:rows, :], low, ((1,), (0,)))
    total = total.reshape(members, steps, INNER, narrow, total.shape[1])
    for g in range(members):
        for j in range(steps):
            sends[j][g, 0] = total[g, j, 0]
            kept_ref[j, g, 0] = total[g, j, 1]


def panel_terms(table, inverse, pieces, ratio):
    members, width, rows = pieces[0].shape
    count = len(pieces)
    steps = table.shape[1] // INNER
    narrow = width // ratio
    half = inverse.shape[1] // 2
    block = column_block(half)
    tiles = half // block
    lefts = members * steps * INNER * narrow
    whole = pl.BlockSpec((members, width, rows), lambda h, n, table: (0, 0, 0))
    flops = 6 * lefts * inverse.size
    outs = pl.pallas_call(
        functools.partial(terms_kernel, (count, ratio, narrow, steps, members)),
        grid_spec=pltpu.PrefetchScalarGridSpec(
            num_scalar_prefetch=1,
            grid=(2, tiles),
            in_specs=[pl.BlockSpec((rows, block), lambda h, n, table: (0, h * tiles + n))] + [whole] * count,
            out_specs=[pl.BlockSpec((members, 1, narrow, block), lambda h, n, table: (0, h, 0, n))] * steps
            + [pl.BlockSpec((steps, members, 1, narrow, block), lambda h, n, table: (0, 0, h, 0, n))],
            scratch_shapes=[
                pltpu.VMEM((count * ratio, members, narrow, rows), jnp.bfloat16),
                pltpu.VMEM((count * ratio, members, narrow, rows), jnp.bfloat16),
                pltpu.VMEM((2 * lefts, rows), jnp.bfloat16),
            ],
        ),
        out_shape=[jax.ShapeDtypeStruct((members, 2, narrow, half), jnp.float32)] * steps
        + [jax.ShapeDtypeStruct((steps, members, 2, narrow, half), jnp.float32)],
        compiler_params=pltpu.CompilerParams(vmem_limit_bytes=32 << 20),
        cost_estimate=pl.CostEstimate(flops=flops, bytes_accessed=4 * inverse.size, transcendentals=0),
        name="panel_terms",
    )(table, inverse, *pieces)
    return outs[:steps], outs[steps]


def gather_pieces(block):
    count = lax.axis_size("col")
    pieces = {0: block}
    for bit in reversed(range(count.bit_length() - 1)):
        for held, piece in list(pieces.items()):
            pieces[held ^ (1 << bit)] = swap_bit(piece, "col", bit)
    return [pieces[i] for i in range(count)]


def mirror_routes(row_count, col_count, shift):
    ratio = row_count // col_count
    straight, first, second = [], [], []
    for r in range(row_count):
        for c in range(col_count):
            target = (c * ratio + (r % ratio + shift) % ratio, r // ratio)
            middle = (r, target[1] // 2 * 2 + c % 2)
            if shift == 0 or middle[1] == c:
                straight.append(((r, c), target))
            else:
                first.append(((r, c), middle))
                second.append((middle, target))
    if len(set(m for _, m in first)) != len(first):
        straight += [(f[0], s[1]) for f, s in zip(first, second)]
        first, second = [], []
    flat = lambda pairs: [(a[0] * col_count + a[1], b[0] * col_count + b[1]) for a, b in pairs]
    return flat(straight), flat(first), flat(second)


def mirrored(pieces):
    row_count = lax.axis_size("row")
    col_count = lax.axis_size("col")
    ratio = row_count // col_count
    lower = lax.axis_index("row") % ratio
    arrived = []
    for shift in range(ratio):
        straight, first, second = mirror_routes(row_count, col_count, shift)
        piece = pieces[(0 + shift) % ratio]
        for l in range(1, ratio):
            piece = jnp.where(lower == l, pieces[(l + shift) % ratio], piece)
        got = lax.ppermute(piece, ("row", "col"), straight)
        if first:
            halfway = lax.ppermute(piece, ("row", "col"), first)
            got = got + lax.ppermute(halfway, ("row", "col"), second)
        arrived.append(got)
    return arrived


def unmirror(arrived, axis):
    ratio = len(arrived)
    lower = lax.axis_index("row") % ratio
    placed = []
    for source in range(ratio):
        piece = arrived[(0 - source) % ratio]
        for l in range(1, ratio):
            piece = jnp.where(lower == l, arrived[(l - source) % ratio], piece)
        placed.append(piece)
    return jnp.concatenate(placed, axis=axis)


def diag_kernel(count, column_ref, *refs):
    pieces, out_ref = refs[:count], refs[count]
    width = pieces[0].shape[1]
    for g in range(out_ref.shape[0]):
        high, low = split(column_ref[g])
        for m in range(count):
            left_high, left_low = split(pieces[m][g])
            left = jnp.concatenate([left_high, left_low], axis=0)
            both = dot(left, high, ((1,), (1,)))
            out_ref[g, m] = both[:width] + both[width:] + dot(left_high, low, ((1,), (1,)))


def diag_terms(column, pieces):
    members, width, rows = column.shape
    count = len(pieces)
    return pl.pallas_call(
        functools.partial(diag_kernel, count),
        out_shape=jax.ShapeDtypeStruct((members, count, width, width), jnp.float32),
        compiler_params=pltpu.CompilerParams(vmem_limit_bytes=16 << 20),
        cost_estimate=pl.CostEstimate(
            flops=6 * members * count * width * width * rows,
            bytes_accessed=4 * members * (count + 1) * width * rows,
            transcendentals=0,
        ),
        name="diag_terms",
    )(column, *pieces)


def on_device(resident_inverse, factor_panel, diag_inverse, ancestors, start_order):
    row_count = lax.axis_size("row")
    col_count = lax.axis_size("col")
    row_index = lax.axis_index("row")
    col_index = lax.axis_index("col")
    rows_here, cols_here = resident_inverse.shape
    sections, _, slice_width = factor_panel.shape
    tile = rows_here * row_count // ancestors.shape[1]
    ratio = row_count // col_count
    narrow = slice_width // ratio
    steps = row_count // INNER
    outer = row_index // INNER
    inner = row_index % INNER
    half = cols_here // 2

    first_tile = (row_index * (rows_here // tile)).astype(jnp.int32).reshape(1)
    own = masked_panels(jnp.swapaxes(factor_panel, 1, 2), ancestors, start_order, first_tile, tile)

    tiles_here = cols_here // tile
    flags = lax.dynamic_slice_in_dim(ancestors, col_index * tiles_here, tiles_here, 1)
    flags = jnp.where((start_order == 0)[:, None], flags[:1], flags[1:]) if sections == 2 else flags[start_order]
    col_masks = jnp.repeat(flags.astype(jnp.float32), tile, axis=1)

    turns = jnp.arange(steps)
    outers = jnp.stack([(outer - 1 - turns) % steps, (outer + 1 + turns) % steps])
    rows_wanted = outers[:, :, None] * INNER + jnp.stack([1 - inner, inner])[None, None, :]
    table = ((rows_wanted // ratio) ^ col_index) * ratio + rows_wanted % ratio
    table = table.reshape(2, steps * INNER).astype(jnp.int32)

    forward = [(r, (r + INNER) % row_count) for r in range(row_count)]
    backward = [(b, a) for a, b in forward]
    across = [(r, r ^ 1) for r in range(row_count)]

    gathered = [gather_pieces(own[s : s + 1]) for s in range(sections)]

    row_results, col_results, diag_parts = [], [], []
    for s, pieces in enumerate(gathered):
        sends, kept = panel_terms(table, resident_inverse, pieces, ratio)
        carry = [None, None]
        for step in range(steps):
            arrived = lax.ppermute(sends[step], "row", across)
            for h in range(2):
                here = kept[step, :, h] + arrived[:, h]
                if step:
                    ring = forward if h == 0 else backward
                    here = here + lax.ppermute(carry[h], "row", ring)
                carry[h] = here
        masks = col_masks[s : s + 1, None, :]
        finished = [-carry[h] * masks[:, :, h * half : (h + 1) * half] for h in range(2)]
        if ratio == 2:
            turned = mirrored(finished)
        else:
            joined = jnp.concatenate(finished, axis=-1)
            turned = mirrored([joined[:, :, q * rows_here : (q + 1) * rows_here] for q in range(ratio)])
        row_results.append(jnp.concatenate(finished, axis=-1))
        column = unmirror(turned, 1)
        col_results.append(column)
        diag_parts.append(diag_terms(column, pieces))

    rest = jnp.concatenate(diag_parts, axis=0).reshape(sections, row_count, narrow, slice_width)
    place = ((row_index // ratio) ^ col_index) * ratio + row_index % ratio
    for bit in range(row_count.bit_length() - 1):
        own_bit = (place >> bit) & 1
        shaped = rest.reshape(sections, -1, 2, narrow, slice_width)
        outgoing = lax.dynamic_index_in_dim(shaped, 1 - own_bit, 2, keepdims=False)
        stays = lax.dynamic_index_in_dim(shaped, own_bit, 2, keepdims=False)
        rest = stays + swap_bit(outgoing, "row", bit)
    if sections == 2:
        flipped = jnp.flip(diag_inverse, axis=0)
        sectioned_diag = jnp.where(start_order[0] == 0, diag_inverse, flipped)
    else:
        sectioned_diag = jnp.take(diag_inverse, start_order, axis=0)
    diag_result = sectioned_diag - rest.reshape(sections, narrow, slice_width)

    col_out = jnp.swapaxes(jnp.concatenate(col_results, axis=0), 1, 2)
    return (col_out, jnp.concatenate(row_results, axis=0), diag_result)


def solution(mesh):
    return jax.shard_map(
        on_device,
        mesh=mesh,
        in_specs=(P("row", "col"), P(None, "row", "col"), P(None, "row", "col"), P(), P()),
        out_specs=(P(None, "row", "col"), P(None, "row", "col"), P(None, "row", "col")),
        check_vma=False,
    )
```

```python
import functools
import math
import jax
import jax.numpy as jnp
from jax import lax
from jax.experimental import pallas as pl
from jax.experimental.pallas import tpu as pltpu
from jax.sharding import PartitionSpec as P

INNER = 2


def swap_bit(block, axis, bit):
    count = lax.axis_size(axis)
    return lax.ppermute(block, axis, [(i, i ^ (1 << bit)) for i in range(count)])


def split(values):
    high = values.astype(jnp.bfloat16)
    return high, (values - high.astype(jnp.float32)).astype(jnp.bfloat16)


def dot(left, right, contract):
    return lax.dot_general(left, right, (contract, ((), ())), preferred_element_type=jnp.float32)


def column_block(columns):
    return next(columns // t for t in range(1, columns + 1) if columns % t == 0 and columns // t <= 512)


def terms_kernel(dims, table_ref, flags_ref, place_ref, inverse_ref, *refs):
    pieces_count, ratio, narrow, steps, members, node, tile = dims
    pieces, refs = refs[:pieces_count], refs[pieces_count:]
    sends, (kept_ref, high_ref, low_ref, left_ref) = refs[:steps], refs[steps:]
    h = pl.program_id(0)
    n = pl.program_id(1)
    rows = members * steps * INNER * narrow

    @pl.when((h == 0) & (n == 0))
    def _():
        for m in range(pieces_count):
            for g in range(members):
                for t in range(left_ref.shape[1] // tile):
                    at = slice(t * tile, (t + 1) * tile)
                    flag = flags_ref[node + g, place_ref[0] + t].astype(jnp.float32)
                    for l in range(ratio):
                        high, low = split(pieces[m][g, l * narrow : (l + 1) * narrow, at] * flag)
                        high_ref[m * ratio + l, g, :, at] = high
                        low_ref[m * ratio + l, g, :, at] = low

    @pl.when(n == 0)
    def _():
        for j in range(steps):
            for i in range(INNER):
                unit = table_ref[h, j * INNER + i]
                for g in range(members):
                    at = ((g * steps + j) * INNER + i) * narrow
                    left_ref[at : at + narrow, :] = high_ref[unit, g]
                    left_ref[rows + at : rows + at + narrow, :] = low_ref[unit, g]

    high, low = split(inverse_ref[...])
    both = dot(left_ref[...], high, ((1,), (0,)))
    total = both[:rows] + both[rows:] + dot(left_ref[:rows, :], low, ((1,), (0,)))
    columns = total.shape[1]
    chunk = math.gcd(columns, tile)
    start = (h * pl.num_programs(1) + n) * columns
    total = total.reshape(members, steps, INNER, narrow, columns)
    for g in range(members):
        for k in range(0, columns, chunk):
            factor = -flags_ref[node + g, place_ref[1] + (start + k) // tile].astype(jnp.float32)
            for j in range(steps):
                sends[j][g, 0, :, k : k + chunk] = total[g, j, 0, :, k : k + chunk] * factor
                kept_ref[j, g, 0, :, k : k + chunk] = total[g, j, 1, :, k : k + chunk] * factor


def panel_terms(node, table, flags, place, inverse, pieces, ratio, tile):
    members, width, rows = pieces[0].shape
    count = len(pieces)
    steps = table.shape[1] // INNER
    narrow = width // ratio
    half = inverse.shape[1] // 2
    block = column_block(half)
    tiles = half // block
    lefts = members * steps * INNER * narrow
    whole = pl.BlockSpec((members, width, rows), lambda h, n, table, flags, place: (0, 0, 0))
    flops = 6 * lefts * inverse.size
    outs = pl.pallas_call(
        functools.partial(terms_kernel, (count, ratio, narrow, steps, members, node, tile)),
        grid_spec=pltpu.PrefetchScalarGridSpec(
            num_scalar_prefetch=3,
            grid=(2, tiles),
            in_specs=[pl.BlockSpec((rows, block), lambda h, n, table, flags, place: (0, h * tiles + n))] + [whole] * count,
            out_specs=[pl.BlockSpec((members, 1, narrow, block), lambda h, n, table, flags, place: (0, h, 0, n))] * steps
            + [pl.BlockSpec((steps, members, 1, narrow, block), lambda h, n, table, flags, place: (0, 0, h, 0, n))],
            scratch_shapes=[
                pltpu.VMEM((count * ratio, members, narrow, rows), jnp.bfloat16),
                pltpu.VMEM((count * ratio, members, narrow, rows), jnp.bfloat16),
                pltpu.VMEM((2 * lefts, rows), jnp.bfloat16),
            ],
        ),
        out_shape=[jax.ShapeDtypeStruct((members, 2, narrow, half), jnp.float32)] * steps
        + [jax.ShapeDtypeStruct((steps, members, 2, narrow, half), jnp.float32)],
        compiler_params=pltpu.CompilerParams(vmem_limit_bytes=32 << 20),
        cost_estimate=pl.CostEstimate(flops=flops, bytes_accessed=4 * inverse.size, transcendentals=0),
        name="panel_terms",
    )(table, flags, place, inverse, *pieces)
    return outs[:steps], outs[steps]


def gather_pieces(block):
    count = lax.axis_size("col")
    pieces = {0: block}
    for bit in reversed(range(count.bit_length() - 1)):
        for held, piece in list(pieces.items()):
            pieces[held ^ (1 << bit)] = swap_bit(piece, "col", bit)
    return [pieces[i] for i in range(count)]


def mirror_routes(row_count, col_count, shift):
    ratio = row_count // col_count
    straight, first, second = [], [], []
    for r in range(row_count):
        for c in range(col_count):
            target = (c * ratio + (r % ratio + shift) % ratio, r // ratio)
            middle = (r, target[1] // 2 * 2 + c % 2)
            if shift == 0 or middle[1] == c:
                straight.append(((r, c), target))
            else:
                first.append(((r, c), middle))
                second.append((middle, target))
    if len(set(m for _, m in first)) != len(first):
        straight += [(f[0], s[1]) for f, s in zip(first, second)]
        first, second = [], []
    flat = lambda pairs: [(a[0] * col_count + a[1], b[0] * col_count + b[1]) for a, b in pairs]
    return flat(straight), flat(first), flat(second)


def mirrored(pieces):
    row_count = lax.axis_size("row")
    col_count = lax.axis_size("col")
    ratio = row_count // col_count
    lower = lax.axis_index("row") % ratio
    arrived = []
    for shift in range(ratio):
        straight, first, second = mirror_routes(row_count, col_count, shift)
        piece = pieces[(0 + shift) % ratio]
        for l in range(1, ratio):
            piece = jnp.where(lower == l, pieces[(l + shift) % ratio], piece)
        got = lax.ppermute(piece, ("row", "col"), straight)
        if first:
            halfway = lax.ppermute(piece, ("row", "col"), first)
            got = got + lax.ppermute(halfway, ("row", "col"), second)
        arrived.append(got)
    return arrived


def unmirror(arrived, axis):
    ratio = len(arrived)
    lower = lax.axis_index("row") % ratio
    placed = []
    for source in range(ratio):
        piece = arrived[(0 - source) % ratio]
        for l in range(1, ratio):
            piece = jnp.where(lower == l, arrived[(l - source) % ratio], piece)
        placed.append(piece)
    return jnp.concatenate(placed, axis=axis)


def diag_kernel(count, column_ref, *refs):
    pieces, out_ref = refs[:count], refs[count]
    width = pieces[0].shape[1]
    for g in range(out_ref.shape[0]):
        high, low = split(column_ref[g])
        for m in range(count):
            left_high, left_low = split(pieces[m][g])
            left = jnp.concatenate([left_high, left_low], axis=0)
            both = dot(left, high, ((1,), (1,)))
            out_ref[g, m] = both[:width] + both[width:] + dot(left_high, low, ((1,), (1,)))


def diag_terms(column, pieces):
    members, width, rows = column.shape
    count = len(pieces)
    return pl.pallas_call(
        functools.partial(diag_kernel, count),
        out_shape=jax.ShapeDtypeStruct((members, count, width, width), jnp.float32),
        compiler_params=pltpu.CompilerParams(vmem_limit_bytes=16 << 20),
        cost_estimate=pl.CostEstimate(
            flops=6 * members * count * width * width * rows,
            bytes_accessed=4 * members * (count + 1) * width * rows,
            transcendentals=0,
        ),
        name="diag_terms",
    )(column, *pieces)


def on_device(resident_inverse, factor_panel, diag_inverse, ancestors, start_order):
    row_count = lax.axis_size("row")
    col_count = lax.axis_size("col")
    row_index = lax.axis_index("row")
    col_index = lax.axis_index("col")
    rows_here, cols_here = resident_inverse.shape
    sections, _, slice_width = factor_panel.shape
    tile = rows_here * row_count // ancestors.shape[1]
    ratio = row_count // col_count
    narrow = slice_width // ratio
    steps = row_count // INNER
    outer = row_index // INNER
    inner = row_index % INNER

    place = jnp.stack([row_index * (rows_here // tile), col_index * cols_here // tile]).astype(jnp.int32)
    panel = jnp.swapaxes(factor_panel, 1, 2)

    turns = jnp.arange(steps)
    outers = jnp.stack([(outer - 1 - turns) % steps, (outer + 1 + turns) % steps])
    rows_wanted = outers[:, :, None] * INNER + jnp.stack([1 - inner, inner])[None, None, :]
    table = ((rows_wanted // ratio) ^ col_index) * ratio + rows_wanted % ratio
    table = table.reshape(2, steps * INNER).astype(jnp.int32)

    forward = [(r, (r + INNER) % row_count) for r in range(row_count)]
    backward = [(b, a) for a, b in forward]
    across = [(r, r ^ 1) for r in range(row_count)]

    gathered = [gather_pieces(panel[s : s + 1]) for s in range(sections)]

    row_results, col_results, diag_parts = [], [], []
    for s, pieces in enumerate(gathered):
        sends, kept = panel_terms(s, table, ancestors, place, resident_inverse, pieces, ratio, tile)
        carry = [None, None]
        for step in range(steps):
            arrived = lax.ppermute(sends[step], "row", across)
            for h in range(2):
                here = kept[step, :, h] + arrived[:, h]
                if step:
                    ring = forward if h == 0 else backward
                    here = here + lax.ppermute(carry[h], "row", ring)
                carry[h] = here
        finished = carry
        if ratio == 2:
            turned = mirrored(finished)
        else:
            joined = jnp.concatenate(finished, axis=-1)
            turned = mirrored([joined[:, :, q * rows_here : (q + 1) * rows_here] for q in range(ratio)])
        row_results.append(jnp.concatenate(finished, axis=-1))
        column = unmirror(turned, 1)
        col_results.append(column)
        diag_parts.append(diag_terms(column, pieces))

    rest = jnp.concatenate(diag_parts, axis=0).reshape(sections, row_count, narrow, slice_width)
    spot = ((row_index // ratio) ^ col_index) * ratio + row_index % ratio
    for bit in range(row_count.bit_length() - 1):
        own_bit = (spot >> bit) & 1
        shaped = rest.reshape(sections, -1, 2, narrow, slice_width)
        outgoing = lax.dynamic_index_in_dim(shaped, 1 - own_bit, 2, keepdims=False)
        stays = lax.dynamic_index_in_dim(shaped, own_bit, 2, keepdims=False)
        rest = stays + swap_bit(outgoing, "row", bit)
    diag_parts = list(diag_inverse - rest.reshape(sections, narrow, slice_width))
    rows = [block[0] for block in row_results]
    columns = [block[0] for block in col_results]
    in_order = lambda blocks: sectioned(blocks, start_order)
    return (jnp.swapaxes(in_order(columns), 1, 2), in_order(rows), in_order(diag_parts))


def sectioned(blocks, order):
    if len(blocks) == 2:
        straight = order[0] == 0
        return jnp.stack([jnp.where(straight, blocks[0], blocks[1]), jnp.where(straight, blocks[1], blocks[0])])
    return jnp.take(jnp.stack(blocks), order, axis=0)


def solution(mesh):
    return jax.shard_map(
        on_device,
        mesh=mesh,
        in_specs=(P("row", "col"), P(None, "row", "col"), P(None, "row", "col"), P(), P()),
        out_specs=(P(None, "row", "col"), P(None, "row", "col"), P(None, "row", "col")),
        check_vma=False,
    )
```

```python
import functools
import math
import jax
import jax.numpy as jnp
from jax import lax
from jax.experimental import pallas as pl
from jax.experimental.pallas import tpu as pltpu
from jax.sharding import PartitionSpec as P

INNER = 2


def swap_bit(block, axis, bit):
    count = lax.axis_size(axis)
    return lax.ppermute(block, axis, [(i, i ^ (1 << bit)) for i in range(count)])


def split(values):
    high = values.astype(jnp.bfloat16)
    return high, (values - high.astype(jnp.float32)).astype(jnp.bfloat16)


def dot(left, right, contract):
    return lax.dot_general(left, right, (contract, ((), ())), preferred_element_type=jnp.float32)


def column_block(columns):
    return next(columns // t for t in range(1, columns + 1) if columns % t == 0 and columns // t <= 512)


def terms_kernel(dims, table_ref, flags_ref, place_ref, inverse_ref, *refs):
    pieces_count, ratio, narrow, steps, members, node, tile, base = dims
    pieces, refs = refs[:pieces_count], refs[pieces_count:]
    sends, (kept_ref, high_ref, low_ref, left_ref) = refs[:steps], refs[steps:]
    h = pl.program_id(0) + base
    n = pl.program_id(1)
    rows = members * steps * INNER * narrow

    @pl.when((pl.program_id(0) == 0) & (n == 0))
    def _():
        for m in range(pieces_count):
            for g in range(members):
                for t in range(left_ref.shape[1] // tile):
                    at = slice(t * tile, (t + 1) * tile)
                    flag = flags_ref[node + g, place_ref[0] + t].astype(jnp.float32)
                    for l in range(ratio):
                        high, low = split(pieces[m][g, l * narrow : (l + 1) * narrow, at] * flag)
                        high_ref[m * ratio + l, g, :, at] = high
                        low_ref[m * ratio + l, g, :, at] = low

    @pl.when(n == 0)
    def _():
        for j in range(steps):
            for i in range(INNER):
                unit = table_ref[h, j * INNER + i]
                for g in range(members):
                    at = ((g * steps + j) * INNER + i) * narrow
                    left_ref[at : at + narrow, :] = high_ref[unit, g]
                    left_ref[rows + at : rows + at + narrow, :] = low_ref[unit, g]

    high, low = split(inverse_ref[...])
    both = dot(left_ref[...], high, ((1,), (0,)))
    total = both[:rows] + both[rows:] + dot(left_ref[:rows, :], low, ((1,), (0,)))
    columns = total.shape[1]
    chunk = math.gcd(columns, tile)
    start = (h * pl.num_programs(1) + n) * columns
    total = total.reshape(members, steps, INNER, narrow, columns)
    for g in range(members):
        for k in range(0, columns, chunk):
            factor = -flags_ref[node + g, place_ref[1] + (start + k) // tile].astype(jnp.float32)
            for j in range(steps):
                sends[j][g, 0, :, k : k + chunk] = total[g, j, 0, :, k : k + chunk] * factor
                kept_ref[j, g, 0, :, k : k + chunk] = total[g, j, 1, :, k : k + chunk] * factor


def panel_terms(node, table, flags, place, inverse, pieces, ratio, tile, halves):
    members, width, rows = pieces[0].shape
    count = len(pieces)
    steps = table.shape[1] // INNER
    narrow = width // ratio
    half = inverse.shape[1] // 2
    block = column_block(half)
    tiles = half // block
    lefts = members * steps * INNER * narrow
    whole = pl.BlockSpec((members, width, rows), lambda h, n, table, flags, place: (0, 0, 0))
    flops = 3 * len(halves) * lefts * inverse.size
    outs = pl.pallas_call(
        functools.partial(terms_kernel, (count, ratio, narrow, steps, members, node, tile, halves[0])),
        grid_spec=pltpu.PrefetchScalarGridSpec(
            num_scalar_prefetch=3,
            grid=(len(halves), tiles),
            in_specs=[pl.BlockSpec((rows, block), lambda h, n, table, flags, place: (0, (h + halves[0]) * tiles + n))] + [whole] * count,
            out_specs=[pl.BlockSpec((members, 1, narrow, block), lambda h, n, table, flags, place: (0, h, 0, n))] * steps
            + [pl.BlockSpec((steps, members, 1, narrow, block), lambda h, n, table, flags, place: (0, 0, h, 0, n))],
            scratch_shapes=[
                pltpu.VMEM((count * ratio, members, narrow, rows), jnp.bfloat16),
                pltpu.VMEM((count * ratio, members, narrow, rows), jnp.bfloat16),
                pltpu.VMEM((2 * lefts, rows), jnp.bfloat16),
            ],
        ),
        out_shape=[jax.ShapeDtypeStruct((members, len(halves), narrow, half), jnp.float32)] * steps
        + [jax.ShapeDtypeStruct((steps, members, len(halves), narrow, half), jnp.float32)],
        compiler_params=pltpu.CompilerParams(vmem_limit_bytes=(32 if len(halves) == 2 else 46) << 20),
        cost_estimate=pl.CostEstimate(flops=flops, bytes_accessed=2 * len(halves) * inverse.size, transcendentals=0),
        name="panel_terms",
    )(table, flags, place, inverse, *pieces)
    return outs[:steps], outs[steps]


def gather_pieces(block):
    count = lax.axis_size("col")
    pieces = {0: block}
    for bit in reversed(range(count.bit_length() - 1)):
        for held, piece in list(pieces.items()):
            pieces[held ^ (1 << bit)] = swap_bit(piece, "col", bit)
    return [pieces[i] for i in range(count)]


def mirror_routes(row_count, col_count, shift):
    ratio = row_count // col_count
    straight, first, second = [], [], []
    for r in range(row_count):
        for c in range(col_count):
            target = (c * ratio + (r % ratio + shift) % ratio, r // ratio)
            middle = (r, target[1] // 2 * 2 + c % 2)
            if shift == 0 or middle[1] == c:
                straight.append(((r, c), target))
            else:
                first.append(((r, c), middle))
                second.append((middle, target))
    if len(set(m for _, m in first)) != len(first):
        straight += [(f[0], s[1]) for f, s in zip(first, second)]
        first, second = [], []
    flat = lambda pairs: [(a[0] * col_count + a[1], b[0] * col_count + b[1]) for a, b in pairs]
    return flat(straight), flat(first), flat(second)


def mirrored(pieces):
    row_count = lax.axis_size("row")
    col_count = lax.axis_size("col")
    ratio = row_count // col_count
    lower = lax.axis_index("row") % ratio
    arrived = []
    for shift in range(ratio):
        straight, first, second = mirror_routes(row_count, col_count, shift)
        piece = pieces[(0 + shift) % ratio]
        for l in range(1, ratio):
            piece = jnp.where(lower == l, pieces[(l + shift) % ratio], piece)
        got = lax.ppermute(piece, ("row", "col"), straight)
        if first:
            halfway = lax.ppermute(piece, ("row", "col"), first)
            got = got + lax.ppermute(halfway, ("row", "col"), second)
        arrived.append(got)
    return arrived


def unmirror(arrived, axis):
    ratio = len(arrived)
    lower = lax.axis_index("row") % ratio
    placed = []
    for source in range(ratio):
        piece = arrived[(0 - source) % ratio]
        for l in range(1, ratio):
            piece = jnp.where(lower == l, arrived[(l - source) % ratio], piece)
        placed.append(piece)
    return jnp.concatenate(placed, axis=axis)


def diag_kernel(count, column_ref, *refs):
    pieces, out_ref = refs[:count], refs[count]
    width = pieces[0].shape[1]
    for g in range(out_ref.shape[0]):
        high, low = split(column_ref[g])
        for m in range(count):
            left_high, left_low = split(pieces[m][g])
            left = jnp.concatenate([left_high, left_low], axis=0)
            both = dot(left, high, ((1,), (1,)))
            out_ref[g, m] = both[:width] + both[width:] + dot(left_high, low, ((1,), (1,)))


def diag_terms(column, pieces):
    members, width, rows = column.shape
    count = len(pieces)
    return pl.pallas_call(
        functools.partial(diag_kernel, count),
        out_shape=jax.ShapeDtypeStruct((members, count, width, width), jnp.float32),
        compiler_params=pltpu.CompilerParams(vmem_limit_bytes=16 << 20),
        cost_estimate=pl.CostEstimate(
            flops=6 * members * count * width * width * rows,
            bytes_accessed=4 * members * (count + 1) * width * rows,
            transcendentals=0,
        ),
        name="diag_terms",
    )(column, *pieces)


def on_device(resident_inverse, factor_panel, diag_inverse, ancestors, start_order):
    row_count = lax.axis_size("row")
    col_count = lax.axis_size("col")
    row_index = lax.axis_index("row")
    col_index = lax.axis_index("col")
    rows_here, cols_here = resident_inverse.shape
    sections, _, slice_width = factor_panel.shape
    tile = rows_here * row_count // ancestors.shape[1]
    ratio = row_count // col_count
    narrow = slice_width // ratio
    steps = row_count // INNER
    outer = row_index // INNER
    inner = row_index % INNER

    place = jnp.stack([row_index * (rows_here // tile), col_index * cols_here // tile]).astype(jnp.int32)
    panel = jnp.swapaxes(factor_panel, 1, 2)

    turns = jnp.arange(steps)
    outers = jnp.stack([(outer - 1 - turns) % steps, (outer + 1 + turns) % steps])
    rows_wanted = outers[:, :, None] * INNER + jnp.stack([1 - inner, inner])[None, None, :]
    table = ((rows_wanted // ratio) ^ col_index) * ratio + rows_wanted % ratio
    table = table.reshape(2, steps * INNER).astype(jnp.int32)

    forward = [(r, (r + INNER) % row_count) for r in range(row_count)]
    backward = [(b, a) for a, b in forward]
    across = [(r, r ^ 1) for r in range(row_count)]

    gathered = [gather_pieces(panel[s : s + 1]) for s in range(sections)]

    row_results, col_results, diag_parts = [], [], []
    for s, pieces in enumerate(gathered):
        terms = {}
        for halves in [[0], [1]] if s == 0 else [[0, 1]]:
            sends, kept = panel_terms(
                s, table, ancestors, place, resident_inverse, pieces, ratio, tile, halves
            )
            for i, h in enumerate(halves):
                terms[h] = (halves[0], i, sends, kept)
        carry = [None, None]
        for step in range(steps):
            came = {
                base: lax.ppermute(sends[step], "row", across)
                for base, _, sends, _ in terms.values()
                if base == 0 or s == 0
            }
            for h in range(2):
                base, i, _, kept = terms[h]
                here = kept[step, :, i] + came[base][:, i]
                if step:
                    ring = forward if h == 0 else backward
                    here = here + lax.ppermute(carry[h], "row", ring)
                carry[h] = here
        finished = carry
        if ratio == 2:
            turned = mirrored(finished)
        else:
            joined = jnp.concatenate(finished, axis=-1)
            turned = mirrored([joined[:, :, q * rows_here : (q + 1) * rows_here] for q in range(ratio)])
        row_results.append(jnp.concatenate(finished, axis=-1))
        column = unmirror(turned, 1)
        col_results.append(column)
        diag_parts.append(diag_terms(column, pieces))

    rest = jnp.concatenate(diag_parts, axis=0).reshape(sections, row_count, narrow, slice_width)
    spot = ((row_index // ratio) ^ col_index) * ratio + row_index % ratio
    for bit in range(row_count.bit_length() - 1):
        own_bit = (spot >> bit) & 1
        shaped = rest.reshape(sections, -1, 2, narrow, slice_width)
        outgoing = lax.dynamic_index_in_dim(shaped, 1 - own_bit, 2, keepdims=False)
        stays = lax.dynamic_index_in_dim(shaped, own_bit, 2, keepdims=False)
        rest = stays + swap_bit(outgoing, "row", bit)
    diag_parts = list(diag_inverse - rest.reshape(sections, narrow, slice_width))
    rows = [block[0] for block in row_results]
    columns = [block[0] for block in col_results]
    in_order = lambda blocks: sectioned(blocks, start_order)
    return (jnp.swapaxes(in_order(columns), 1, 2), in_order(rows), in_order(diag_parts))


def sectioned(blocks, order):
    if len(blocks) == 2:
        straight = order[0] == 0
        return jnp.stack([jnp.where(straight, blocks[0], blocks[1]), jnp.where(straight, blocks[1], blocks[0])])
    return jnp.take(jnp.stack(blocks), order, axis=0)


def solution(mesh):
    return jax.shard_map(
        on_device,
        mesh=mesh,
        in_specs=(P("row", "col"), P(None, "row", "col"), P(None, "row", "col"), P(), P()),
        out_specs=(P(None, "row", "col"), P(None, "row", "col"), P(None, "row", "col")),
        check_vma=False,
    )
```
